32 devices in a mesh: sect: 4 (over y, x), tile: 8 (over z, core).
Axes of the slice: x: 2, y: 2, z: 4, core: 2. Of those that a mesh axis runs over, the one named last changes fastest.
Arguments:
- zonal: float32 [4, 64, 512], P('sect', 'tile'), may hold values from -1.5 to 1.5
- merid: float32 [4, 64, 512], P('sect', 'tile'), may hold values from -1.5 to 1.5
- height: float32 [4, 64, 512], P('sect', 'tile'), may hold values from -6 to 6
- level_kappa: float32 [4], replicated, may hold values from 0.2 to 2
- sea: int32 [64, 512], P('tile'), may hold values 0 or 1
- flags: int32 [4, 64, 512], P(None, 'tile', 'sect'), may hold values 0 or 1
- conc: float32 [12, 4, 64, 512], P(None, None, 'tile', 'sect'), may hold values from 0.1 to 2
- react: float32 [12, 12], replicated, may hold values from -1.2 to 1.2
- absorb: float32 [12], replicated, may hold values from 0.05 to 1
- light: float32 [4], replicated, may hold values from 0.1 to 1
Outputs:
- conc_out: float32 [12, 4, 64, 512], P(None, None, 'tile', 'sect')
- zonal_out: float32 [4, 64, 512], P('sect', 'tile')
- merid_out: float32 [4, 64, 512], P('sect', 'tile')
- height_out: float32 [4, 64, 512], P('sect', 'tile')
The draws below stay inside these ranges and needn't reach their ends.
All inputs are finite; a program needn't handle non-finite values. No bound on the sum of `sea` or of `flags` on one device may be relied on, other than what follows from the above.
Results may differ from the reference program's by a relative error of at most 0.00022.
Values sent between devices are 32-bit elements; how exact they have to be, the bound alone decides.
A program may use at most 64 MiB of HBM per device.

```python
import math
import jax
import jax.numpy as jnp
from jax import lax

NTR = 12
STEPS = 4
INTERVALS = 2
NZ = 4
NY = 64
NX = 512


def with_ends(entries, rng, least, high):
    dims = entries.shape
    place = [jax.random.randint(jax.random.fold_in(rng, axis), (), 0, dims[axis]) for axis in range(len(dims))]
    entries = entries.at[tuple(place)].set(least)
    longest = dims.index(max(dims))
    place[longest] = (place[longest] + 1) % dims[longest]
    return entries.at[tuple(place)].set(high)


def block_levels(rng, dims, split, smallest, largest):
    def one(axis_at, blocks):
        heights = jax.random.uniform(jax.random.fold_in(jax.random.fold_in(rng, 6), axis_at), (blocks,), jnp.float32, smallest / len(split), largest / len(split))
        return jnp.repeat(jnp.exp(heights), dims[axis_at] // blocks).reshape((-1,) + (1,) * (len(dims) - axis_at - 1))

    level = one(*split[0])
    for cut in split[1:]:
        level = level * one(*cut)
    return level


def gaussian(own_key, extent, deviation, bound, pieces=(), kind=jnp.bfloat16):
    values = deviation * jax.random.normal(own_key, extent, jnp.float32)
    if pieces:
        values = values * block_levels(own_key, extent, pieces, -0.22, 0.18)
    return jnp.clip(values, -bound, bound).astype(kind)


def setup_inputs(seed: int = 0) -> dict:
    key_list = jax.random.split(jax.random.key(seed), 11)
    return {
        "zonal": gaussian(key_list[0], (NZ, NY, NX), 0.3, 1.5, ((0, 4), (1, 8)), jnp.float32),
        "merid": gaussian(key_list[1], (NZ, NY, NX), 0.3, 1.5, ((0, 4), (1, 8)), jnp.float32),
        "height": gaussian(key_list[2], (NZ, NY, NX), 1.0, 6.0, ((0, 4), (1, 8)), jnp.float32),
        "level_kappa": jnp.clip(jnp.exp(jax.random.uniform(key_list[3], (NZ,), jnp.float32, math.log(0.2), math.log(2.0))), 0.2, 2.0),
        "sea": with_ends((jax.random.randint(key_list[4], (NY, NX), 0, 8) < 7).astype(jnp.int32), jax.random.fold_in(key_list[4], 1), 0, 1),
        "flags": with_ends((jax.random.randint(key_list[5], (NZ, NY, NX), 0, 2) < 1).astype(jnp.int32), jax.random.fold_in(key_list[5], 1), 0, 1),
        "conc": jnp.clip(jnp.exp(math.log(2.0) - 2.9957323 * jax.random.uniform(key_list[6], (NTR, NZ, NY, NX), jnp.float32) ** block_levels(key_list[6], (NTR, NZ, NY, NX), ((2, 8), (3, 4)), -0.2, 0.2)), 0.1, 2.0),
        "react": gaussian(key_list[7], (NTR, NTR), 0.3, 1.2, (), jnp.float32),
        "absorb": jnp.clip(jnp.exp(jax.random.uniform(key_list[8], (NTR,), jnp.float32, math.log(0.05), math.log(1.0))), 0.05, 1.0),
        "light": jnp.clip(jnp.exp(jax.random.uniform(key_list[9], (NZ,), jnp.float32, math.log(0.1), math.log(1.0))), 0.1, 1.0),
    }


time_step = 0.1
gravity = 1.0
coriolis = 0.3
viscosity = 0.05
heat_coupling = 0.05
tracer_step = 0.5
stir_gain = 4.0


def centred(field, axis):
    return 0.5 * (jnp.roll(field, -1, axis) - jnp.roll(field, 1, axis))


def laplace(field):
    total = jnp.roll(field, -1, 1) + jnp.roll(field, 1, 1)
    total = total + jnp.roll(field, -1, 2) + jnp.roll(field, 1, 2)
    return total - 4.0 * field


def upwind(conc, speed, flag, axis):
    ahead = jnp.roll(conc, -1, axis)
    behind = jnp.roll(conc, 1, axis)
    upper = jnp.maximum(speed, 0.0) * (conc - behind) + jnp.minimum(speed, 0.0) * (ahead - conc)
    middle = 0.5 * speed * (ahead - behind)
    return jnp.where(flag == 1, upper, middle)


def column_solve(starred, kappa):
    levels = starred.shape[1]
    couple = [tracer_step * 0.5 * (kappa[k] + kappa[k + 1]) for k in range(levels - 1)]
    factor = []
    partial_rhs = []
    for k in range(levels):
        lower = couple[k - 1] if k > 0 else jnp.zeros_like(kappa[0])
        upper = couple[k] if k < levels - 1 else jnp.zeros_like(kappa[0])
        diagonal = 1.0 + lower + upper
        if k == 0:
            denom = diagonal
            rhs_now = starred[:, 0] / denom
        else:
            denom = diagonal + lower * factor[k - 1]
            rhs_now = (starred[:, k] + lower * partial_rhs[k - 1]) / denom
        factor.append(-upper / denom)
        partial_rhs.append(rhs_now)
    result = [None] * levels
    result[levels - 1] = partial_rhs[levels - 1]
    for k in range(levels - 2, -1, -1):
        result[k] = partial_rhs[k] - factor[k] * result[k + 1]
    return jnp.stack(result, axis=1)


def reference(zonal, merid, height, level_kappa, sea, flags, conc, react, absorb, light):
    wet = sea.astype(jnp.float32)
    forcing = jnp.zeros(height.shape, jnp.float32)
    for interval in range(INTERVALS):
        zonal_sum = jnp.zeros(zonal.shape, jnp.float32)
        merid_sum = jnp.zeros(merid.shape, jnp.float32)
        for step in range(STEPS):
            height = height - time_step * (centred(zonal, 2) + centred(merid, 1)) + time_step * heat_coupling * forcing
            zonal_new = wet * (zonal + time_step * (coriolis * merid - gravity * centred(height, 2) + viscosity * laplace(zonal)))
            merid_new = wet * (merid + time_step * (-coriolis * zonal - gravity * centred(height, 1) + viscosity * laplace(merid)))
            zonal, merid = zonal_new, merid_new
            zonal_sum = zonal_sum + zonal
            merid_sum = merid_sum + merid
        zonal_mean = zonal_sum / STEPS
        merid_mean = merid_sum / STEPS
        kappa = level_kappa[:, None, None] * (1.0 + stir_gain * (zonal_mean * zonal_mean + merid_mean * merid_mean))
        moving = upwind(conc, zonal_mean, flags, 3) + upwind(conc, merid_mean, flags, 2)
        starred = conc - tracer_step * wet * moving
        mixed = column_solve(starred, kappa)
        growth = jnp.einsum("ij,jzyx->izyx", react, mixed, precision=lax.Precision.HIGHEST)
        conc = mixed + tracer_step * wet * growth
        if interval + 1 < INTERVALS:
            forcing = light[:, None, None] * jnp.einsum("k,kzyx->zyx", absorb, conc, precision=lax.Precision.HIGHEST)
    return conc, zonal, merid, height
```

```python
import functools

import jax
import jax.numpy as jnp
from jax import lax
from jax.experimental import pallas as pl
from jax.experimental.pallas import tpu as pltpu
from jax.sharding import PartitionSpec as P

STEPS = 4
INTERVALS = 2

time_step = 0.1
gravity = 1.0
coriolis = 0.3
viscosity = 0.05
heat_coupling = 0.05
tracer_step = 0.5
stir_gain = 4.0

LANES = 128


def ocean_steps(zonal, merid, height, wet, forcing, rows):
    tall, wide = zonal.shape

    def east(a):
        return pltpu.roll(a, wide - 1, 1)

    def west(a):
        return pltpu.roll(a, 1, 1)

    def north(a):
        return pltpu.roll(a, tall - 1, 0)

    def south(a):
        return pltpu.roll(a, 1, 0)

    own = slice(rows, 2 * rows)
    zonal_sum = jnp.zeros((rows, wide), jnp.float32)
    merid_sum = jnp.zeros((rows, wide), jnp.float32)
    for _ in range(STEPS):
        ze, zw, zn, zs = east(zonal), west(zonal), north(zonal), south(zonal)
        me, mw, mn, ms = east(merid), west(merid), north(merid), south(merid)
        height = height - (0.5 * time_step) * ((ze - zw) + (mn - ms))
        if forcing is not None:
            height = height + (time_step * heat_coupling) * forcing
        zonal_lap = zn + zs + ze + zw - 4.0 * zonal
        merid_lap = mn + ms + me + mw - 4.0 * merid
        zonal_new = wet * (
            zonal
            + time_step
            * (
                coriolis * merid
                - (0.5 * gravity) * (east(height) - west(height))
                + viscosity * zonal_lap
            )
        )
        merid_new = wet * (
            merid
            + time_step
            * (
                -coriolis * zonal
                - (0.5 * gravity) * (north(height) - south(height))
                + viscosity * merid_lap
            )
        )
        zonal, merid = zonal_new, merid_new
        zonal_sum = zonal_sum + zonal[own]
        merid_sum = merid_sum + merid[own]
    return zonal[own], merid[own], height[own], zonal_sum / STEPS, merid_sum / STEPS


def kernel(
    sects,
    tiles,
    zonal_in,
    merid_in,
    height_in,
    sea_in,
    flags_in,
    conc_in,
    kappa_in,
    react_in,
    absorb_in,
    light_in,
    conc_out,
    zonal_out,
    merid_out,
    height_out,
    ocean,
    sea,
    flags,
    conc,
    react_d,
    base,
    west_v,
    east_v,
    south_v,
    north_v,
    cols_send,
    cols_recv,
    rows_send,
    rows_recv,
    state_send,
    mean_send,
    mean_recv,
    heat_send,
    heat_recv,
    local_sem,
    first_send,
    first_recv,
    state_ssem,
    state_rsem,
    halo_ssem,
    halo_rsem,
    mean_ssem,
    mean_rsem,
    heat_ssem,
    heat_rsem,
):
    me_s = lax.axis_index("sect")
    me_t = lax.axis_index("tile")
    tracers, levels, rows, columns = conc_in.shape
    depth = zonal_in.shape[0]
    above = lax.rem(me_t + 1, tiles)
    below = lax.rem(me_t + tiles - 1, tiles)
    steps_t = {1: above, 0: me_t, -1: below}

    def sect_at(offset):
        return lax.rem(me_s + offset, sects)

    def remote(src, dst, send, recv, to_s, to_t):
        return pltpu.make_async_remote_copy(
            src_ref=src,
            dst_ref=dst,
            send_sem=send,
            recv_sem=recv,
            device_id=(to_s, to_t),
            device_id_type=pl.DeviceIdType.MESH,
        )

    def slot(step):
        return pl.ds((1 - step) * rows, rows)

    fields_in = (zonal_in, merid_in, height_in)
    local = [
        pltpu.make_async_copy(conc_in, conc, local_sem.at[0]),
        pltpu.make_async_copy(flags_in, flags, local_sem.at[1]),
        pltpu.make_async_copy(sea_in, sea.at[slot(0)], local_sem.at[2]),
    ] + [
        pltpu.make_async_copy(field, ocean.at[0, f, :, slot(0)], local_sem.at[3 + f])
        for f, field in enumerate(fields_in)
    ]
    barrier = pltpu.get_barrier_semaphore()
    peers = [(o, d) for o in range(sects) for d in (1, -1, 0) if (o, d) != (0, 0)]
    for o, d in peers:
        pl.semaphore_signal(
            barrier,
            inc=1,
            device_id=(sect_at(o), steps_t[d]),
            device_id_type=pl.DeviceIdType.MESH,
        )
    for copy in local:
        copy.start()
    pl.semaphore_wait(barrier, len(peers))

    first = []
    for i, d in enumerate((1, -1)):
        for f, field in enumerate(fields_in):
            first.append(
                remote(
                    field,
                    ocean.at[0, f, :, slot(d)],
                    first_send.at[i, f],
                    first_recv.at[i, f],
                    me_s,
                    steps_t[d],
                )
            )
        first.append(
            remote(
                sea_in,
                sea.at[slot(d)],
                first_send.at[i, 3],
                first_recv.at[i, 3],
                me_s,
                steps_t[d],
            )
        )
    for copy in first:
        copy.start()
    sent = list(first)

    lane = lax.broadcasted_iota(jnp.int32, (rows, columns), 1)
    row = lax.broadcasted_iota(jnp.int32, (rows, columns), 0)

    for copy in local[:3]:
        copy.wait()
    own_columns = pl.ds(pl.multiple_of(me_s * columns, LANES), columns)
    sea_cols = sea[slot(0), own_columns]
    wet_cols = sea_cols.astype(jnp.float32)
    is_wet = sea_cols == 1

    def react_and_send(turn, heated):
        names = tracers + (1 if heated else 0)
        cells = names * levels
        to_east = [jnp.zeros((rows, columns), jnp.float32) for _ in range(pl.cdiv(cells, LANES))]
        to_west = list(to_east)
        for k in range(levels):
            old = [conc[i, k] for i in range(tracers)]
            heat_d = None
            for i in range(names):
                n = i * levels + k
                if i < tracers:
                    growth = react_in[i, 0] * old[0]
                    for j in range(1, tracers):
                        growth = growth + react_in[i, j] * old[j]
                    new = old[i] + tracer_step * growth
                    kept = jnp.where(is_wet, new, old[i])
                    if heated:
                        a = absorb_in[i]
                        heat_d = a * new if i == 0 else heat_d + a * new
                        heat_b = a * kept if i == 0 else heat_b + a * kept
                else:
                    new, kept = heat_d, heat_b
                react_d[n] = new
                base[n] = kept
                rows_send[turn, 0, pl.ds(n, 1)] = new[rows - 1 : rows]
                rows_send[turn, 1, pl.ds(n, 1)] = new[0:1]
                p, at = divmod(n, LANES)
                here = lane == at
                turned = pltpu.roll(new, (at + 1) % columns, 1)
                to_east[p] = jnp.where(here, turned, to_east[p])
                turned = pltpu.roll(new, at, 1) if at else new
                to_west[p] = jnp.where(here, turned, to_west[p])
        for p in range(len(to_east)):
            cols_send[turn, 0, p] = to_east[p]
            cols_send[turn, 1, p] = to_west[p]
        copies = []
        for i, d in enumerate((1, -1)):
            copies.append(
                remote(
                    rows_send.at[turn, i],
                    rows_recv.at[turn, i],
                    halo_ssem.at[turn, i],
                    halo_rsem.at[turn, i],
                    me_s,
                    steps_t[d],
                )
            )
            copies.append(
                remote(
                    cols_send.at[turn, i],
                    cols_recv.at[turn, i],
                    halo_ssem.at[turn, 2 + i],
                    halo_rsem.at[turn, 2 + i],
                    sect_at(1 if i == 0 else sects - 1),
                    me_t,
                )
            )
        for copy in copies:
            copy.start()
        sent.extend(copies)
        return copies, cells

    def shift_cells(turn, cells):
        from_west = [cols_recv[turn, 0, p] for p in range(pl.cdiv(cells, LANES))]
        from_east = [cols_recv[turn, 1, p] for p in range(pl.cdiv(cells, LANES))]
        for n in range(cells):
            p, at = divmod(n, LANES)
            new = react_d[n]
            edge = pltpu.roll(from_west[p], columns - at, 1) if at else from_west[p]
            west_v[n] = jnp.where(lane == 0, edge, pltpu.roll(new, 1, 1))
            edge = pltpu.roll(from_east[p], columns - 1 - at, 1) if at < columns - 1 else from_east[p]
            east_v[n] = jnp.where(lane == columns - 1, edge, pltpu.roll(new, columns - 1, 1))
            edge = jnp.broadcast_to(rows_recv[turn, 0, pl.ds(n, 1)], (rows, columns))
            south_v[n] = jnp.where(row == 0, edge, pltpu.roll(new, 1, 0))
            edge = jnp.broadcast_to(rows_recv[turn, 1, pl.ds(n, 1)], (rows, columns))
            north_v[n] = jnp.where(row == rows - 1, edge, pltpu.roll(new, rows - 1, 0))

    def send_means(turn, means):
        copies = []
        for l, pair in enumerate(means):
            for f, mean in enumerate(pair):
                for s in range(sects):
                    mean_send[turn, s, f, l] = mean[:, s * columns : (s + 1) * columns]
        for o in range(1, sects):
            to = sect_at(o)
            copies.append(
                remote(
                    mean_send.at[turn, to],
                    mean_recv.at[turn, me_s],
                    mean_ssem.at[turn, o],
                    mean_rsem.at[turn, o],
                    to,
                    me_t,
                )
            )
        for copy in copies:
            copy.start()
        sent.extend(copies)
        mean_recv[turn, me_s] = mean_send[turn, me_s]
        return copies

    def column_terms(turn):
        kappa, stencil = [], []
        half_wet = tracer_step * wet_cols
        for k in range(levels):
            along_x = mean_recv[turn, k // depth, 0, k % depth]
            along_y = mean_recv[turn, k // depth, 1, k % depth]
            kappa.append(kappa_in[k] * (1.0 + stir_gain * (along_x * along_x + along_y * along_y)))
            upwind = flags[k] == 1
            terms = []
            for speed in (along_x, along_y):
                terms.append(half_wet * jnp.where(upwind, jnp.maximum(speed, 0.0), 0.5 * speed))
                terms.append(half_wet * jnp.where(upwind, jnp.minimum(speed, 0.0), 0.5 * speed))
            stencil.append(terms)
        couple = [tracer_step * 0.5 * (kappa[k] + kappa[k + 1]) for k in range(levels - 1)]
        out, factor = [], None
        for k in range(levels):
            denom = 1.0
            if k > 0:
                denom = denom + couple[k - 1]
            if k < levels - 1:
                denom = denom + couple[k]
            if k > 0:
                denom = denom + couple[k - 1] * factor
            inverse = 1.0 / denom
            px, qx, py, qy = stencil[k]
            out.append(
                dict(
                    centre=inverse * (1.0 - ((px - qx) + (py - qy))),
                    west=inverse * px,
                    east=inverse * qx,
                    south=inverse * py,
                    north=inverse * qy,
                    lower=inverse * couple[k - 1] if k > 0 else None,
                    upper=inverse * couple[k] if k < levels - 1 else None,
                )
            )
            factor = -out[k]["upper"] if k < levels - 1 else None
        return out

    def tracer_column(terms, i):
        partial = []
        for k in range(levels):
            n = i * levels + k
            t = terms[k]
            now = (
                t["centre"] * base[n]
                + (t["west"] * west_v[n] - t["east"] * east_v[n])
                + (t["south"] * south_v[n] - t["north"] * north_v[n])
            )
            if k > 0:
                now = now + t["lower"] * partial[k - 1]
            partial.append(now)
        for k in range(levels - 2, -1, -1):
            partial[k] = partial[k] + terms[k]["upper"] * partial[k + 1]
        return partial

    halo0, cells0 = react_and_send(0, True)
    for copy in local[3:]:
        copy.wait()
    for copy in first:
        copy.wait_recv()
    wet = sea[...].astype(jnp.float32)
    means = []
    for l in range(depth):
        z, m, h, zm, mm = ocean_steps(
            ocean[0, 0, l], ocean[0, 1, l], ocean[0, 2, l], wet, None, rows
        )
        means.append((zm, mm))
        for f, value in enumerate((z, m, h)):
            state_send[f, l] = value
    got = send_means(0, means)
    state = []
    for i, d in enumerate((1, -1)):
        state.append(
            remote(
                state_send,
                ocean.at[1, :, :, slot(d)],
                state_ssem.at[i],
                state_rsem.at[i],
                me_s,
                steps_t[d],
            )
        )
    for copy in state:
        copy.start()
    sent.extend(state)
    for f in range(3):
        for l in range(depth):
            ocean[1, f, l, slot(0)] = state_send[f, l]
    for copy in halo0:
        copy.wait_recv()
    shift_cells(0, cells0)
    for copy in got:
        copy.wait_recv()
    terms = column_terms(0)

    heat = tracer_column(terms, tracers)
    for k in range(levels):
        heat_send[k // depth, k % depth] = light_in[k] * heat[k]
    heats = []
    for o in range(sects - 1, -1, -1):
        for i, d in enumerate((1, -1, 0)):
            if (o, d) == (0, 0):
                continue
            to = sect_at(o)
            heats.append(
                remote(
                    heat_send.at[to],
                    heat_recv.at[me_s, :, slot(d)],
                    heat_ssem.at[o, i],
                    heat_rsem.at[o, i],
                    to,
                    steps_t[d],
                )
            )
    for copy in heats:
        copy.start()
    sent.extend(heats)
    heat_recv[me_s, :, slot(0)] = heat_send[me_s]

    for i in range(tracers):
        for k, value in enumerate(tracer_column(terms, i)):
            conc[i, k] = value
    halo1, cells1 = react_and_send(1, False)
    for copy in halo1:
        copy.wait_recv()
    shift_cells(1, cells1)

    for copy in state:
        copy.wait_recv()
    for copy in heats:
        copy.wait_recv()
    means = []
    for l in range(depth):
        forcing = jnp.concatenate([heat_recv[s, l] for s in range(sects)], axis=1)
        z, m, h, zm, mm = ocean_steps(
            ocean[1, 0, l], ocean[1, 1, l], ocean[1, 2, l], wet, forcing, rows
        )
        means.append((zm, mm))
        zonal_out[l] = z
        merid_out[l] = m
        height_out[l] = h
    got = send_means(1, means)
    for copy in got:
        copy.wait_recv()
    terms = column_terms(1)
    for i in range(tracers):
        for k, value in enumerate(tracer_column(terms, i)):
            conc_out[i, k] = value
    for copy in sent:
        copy.wait_send()


def body(sects, tiles, zonal, merid, height, level_kappa, sea, flags, conc, react, absorb, light):
    tracers, levels, rows, columns = conc.shape
    depth, _, wide = zonal.shape
    assert rows >= 2 * STEPS and columns % LANES == 0 and INTERVALS == 2
    cells = (tracers + 1) * levels
    packs = pl.cdiv(cells, LANES)
    padded = pl.cdiv(cells, 8) * 8
    f32 = jnp.float32
    dma = pltpu.SemaphoreType.DMA
    any_space = pl.BlockSpec(memory_space=pl.ANY)
    smem = pl.BlockSpec(memory_space=pltpu.SMEM)
    vmem = pl.BlockSpec(memory_space=pltpu.VMEM)
    return pl.pallas_call(
        functools.partial(kernel, sects, tiles),
        out_shape=[
            jax.ShapeDtypeStruct(conc.shape, f32),
            jax.ShapeDtypeStruct(zonal.shape, f32),
            jax.ShapeDtypeStruct(merid.shape, f32),
            jax.ShapeDtypeStruct(height.shape, f32),
        ],
        in_specs=[any_space] * 6 + [smem] * 4,
        out_specs=[vmem] * 4,
        scratch_shapes=[
            pltpu.VMEM((2, 3, depth, 3 * rows, wide), f32),
            pltpu.VMEM((3 * rows, wide), jnp.int32),
            pltpu.VMEM(flags.shape, jnp.int32),
            pltpu.VMEM(conc.shape, f32),
        ]
        + [pltpu.VMEM((cells, rows, columns), f32)] * 6
        + [
            pltpu.VMEM((2, 2, packs, rows, columns), f32),
            pltpu.VMEM((2, 2, packs, rows, columns), f32),
            pltpu.VMEM((2, 2, padded, columns), f32),
            pltpu.VMEM((2, 2, padded, columns), f32),
            pltpu.VMEM((3, depth, rows, wide), f32),
            pltpu.VMEM((2, sects, 2, depth, rows, columns), f32),
            pltpu.VMEM((2, sects, 2, depth, rows, columns), f32),
            pltpu.VMEM((sects, depth, rows, columns), f32),
            pltpu.VMEM((sects, depth, 3 * rows, columns), f32),
            dma((6,)),
            dma((2, 4)),
            dma((2, 4)),
            dma((2,)),
            dma((2,)),
            dma((2, 4)),
            dma((2, 4)),
            dma((2, sects)),
            dma((2, sects)),
            dma((sects, 3)),
            dma((sects, 3)),
        ],
        compiler_params=pltpu.CompilerParams(collective_id=0, has_side_effects=True),
        name="coupled",
    )(zonal, merid, height, sea, flags, conc, level_kappa, react, absorb, light)


def solution(mesh):
    placed = (
        P("sect", "tile", None),
        P("sect", "tile", None),
        P("sect", "tile", None),
        P(),
        P("tile", None),
        P(None, "tile", "sect"),
        P(None, None, "tile", "sect"),
        P(),
        P(),
        P(),
    )
    return jax.shard_map(
        functools.partial(body, mesh.shape["sect"], mesh.shape["tile"]),
        mesh=mesh,
        in_specs=placed,
        out_specs=(
            P(None, None, "tile", "sect"),
            P("sect", "tile", None),
            P("sect", "tile", None),
            P("sect", "tile", None),
        ),
        check_vma=False,
    )
```

```python
import functools

import jax
import jax.numpy as jnp
from jax import lax
from jax.experimental import pallas as pl
from jax.experimental.pallas import tpu as pltpu
from jax.sharding import PartitionSpec as P

STEPS = 4
INTERVALS = 2

time_step = 0.1
gravity = 1.0
coriolis = 0.3
viscosity = 0.05
heat_coupling = 0.05
tracer_step = 0.5
stir_gain = 4.0

LANES = 128


def ocean_steps(zonal, merid, height, wet, forcing, rows):
    tall, wide = zonal.shape

    def east(a):
        return pltpu.roll(a, wide - 1, 1)

    def west(a):
        return pltpu.roll(a, 1, 1)

    def north(a):
        return pltpu.roll(a, tall - 1, 0)

    def south(a):
        return pltpu.roll(a, 1, 0)

    own = slice(rows, 2 * rows)
    zonal_sum = jnp.zeros((rows, wide), jnp.float32)
    merid_sum = jnp.zeros((rows, wide), jnp.float32)
    for _ in range(STEPS):
        ze, zw, zn, zs = east(zonal), west(zonal), north(zonal), south(zonal)
        me, mw, mn, ms = east(merid), west(merid), north(merid), south(merid)
        height = height - (0.5 * time_step) * ((ze - zw) + (mn - ms))
        if forcing is not None:
            height = height + (time_step * heat_coupling) * forcing
        zonal_lap = zn + zs + ze + zw - 4.0 * zonal
        merid_lap = mn + ms + me + mw - 4.0 * merid
        zonal_new = wet * (
            zonal
            + time_step
            * (
                coriolis * merid
                - (0.5 * gravity) * (east(height) - west(height))
                + viscosity * zonal_lap
            )
        )
        merid_new = wet * (
            merid
            + time_step
            * (
                -coriolis * zonal
                - (0.5 * gravity) * (north(height) - south(height))
                + viscosity * merid_lap
            )
        )
        zonal, merid = zonal_new, merid_new
        zonal_sum = zonal_sum + zonal[own]
        merid_sum = merid_sum + merid[own]
    return zonal[own], merid[own], height[own], zonal_sum / STEPS, merid_sum / STEPS


def kernel(
    sects,
    tiles,
    zonal_in,
    merid_in,
    height_in,
    sea_in,
    flags_in,
    conc_in,
    kappa_hbm,
    react_hbm,
    absorb_hbm,
    light_hbm,
    conc_out,
    zonal_out,
    merid_out,
    height_out,
    kappa_in,
    react_in,
    absorb_in,
    light_in,
    ocean,
    sea,
    flags,
    conc,
    react_d,
    base,
    west_v,
    east_v,
    south_v,
    north_v,
    cols_send,
    cols_recv,
    rows_send,
    rows_recv,
    state_send,
    mean_send,
    mean_recv,
    heat_send,
    heat_recv,
    local_sem,
    first_send,
    first_recv,
    state_ssem,
    state_rsem,
    halo_ssem,
    halo_rsem,
    mean_ssem,
    mean_rsem,
    heat_ssem,
    heat_rsem,
):
    me_s = lax.axis_index("sect")
    me_t = lax.axis_index("tile")
    tracers, levels, rows, columns = conc_in.shape
    depth = zonal_in.shape[0]
    above = lax.rem(me_t + 1, tiles)
    below = lax.rem(me_t + tiles - 1, tiles)
    steps_t = {1: above, 0: me_t, -1: below}

    def sect_at(offset):
        return lax.rem(me_s + offset, sects)

    def remote(src, dst, send, recv, to_s, to_t):
        return pltpu.make_async_remote_copy(
            src_ref=src,
            dst_ref=dst,
            send_sem=send,
            recv_sem=recv,
            device_id=(to_s, to_t),
            device_id_type=pl.DeviceIdType.MESH,
        )

    def slot(step):
        return pl.ds((1 - step) * rows, rows)

    fields_in = (zonal_in, merid_in, height_in)
    local = [
        pltpu.make_async_copy(conc_in, conc, local_sem.at[0]),
        pltpu.make_async_copy(flags_in, flags, local_sem.at[1]),
        pltpu.make_async_copy(sea_in, sea.at[slot(0)], local_sem.at[2]),
    ] + [
        pltpu.make_async_copy(field, ocean.at[0, f, :, slot(0)], local_sem.at[3 + f])
        for f, field in enumerate(fields_in)
    ]
    scalars = [
        pltpu.make_async_copy(src, dst, local_sem.at[6 + i])
        for i, (src, dst) in enumerate(
            (
                (react_hbm, react_in),
                (absorb_hbm, absorb_in),
                (kappa_hbm, kappa_in),
                (light_hbm, light_in),
            )
        )
    ]
    barrier = pltpu.get_barrier_semaphore()
    peers = [(o, d) for o in range(sects) for d in (1, -1, 0) if (o, d) != (0, 0)]
    for o, d in peers:
        pl.semaphore_signal(
            barrier,
            inc=1,
            device_id=(sect_at(o), steps_t[d]),
            device_id_type=pl.DeviceIdType.MESH,
        )
    for copy in scalars + local:
        copy.start()
    pl.semaphore_wait(barrier, len(peers))

    first = []
    for i, d in enumerate((1, -1)):
        for f, field in enumerate(fields_in):
            first.append(
                remote(
                    field,
                    ocean.at[0, f, :, slot(d)],
                    first_send.at[i, f],
                    first_recv.at[i, f],
                    me_s,
                    steps_t[d],
                )
            )
        first.append(
            remote(
                sea_in,
                sea.at[slot(d)],
                first_send.at[i, 3],
                first_recv.at[i, 3],
                me_s,
                steps_t[d],
            )
        )
    for copy in first:
        copy.start()
    sent = list(first)

    lane = lax.broadcasted_iota(jnp.int32, (rows, columns), 1)
    row = lax.broadcasted_iota(jnp.int32, (rows, columns), 0)

    for copy in scalars + local[:3]:
        copy.wait()
    own_columns = pl.ds(pl.multiple_of(me_s * columns, LANES), columns)
    sea_cols = sea[slot(0), own_columns]
    wet_cols = sea_cols.astype(jnp.float32)
    is_wet = sea_cols == 1

    def react_and_send(turn, heated):
        names = tracers + (1 if heated else 0)
        cells = names * levels
        to_east = [jnp.zeros((rows, columns), jnp.float32) for _ in range(pl.cdiv(cells, LANES))]
        to_west = list(to_east)
        for k in range(levels):
            old = [conc[i, k] for i in range(tracers)]
            heat_d = None
            for i in range(names):
                n = i * levels + k
                if i < tracers:
                    growth = react_in[i, 0] * old[0]
                    for j in range(1, tracers):
                        growth = growth + react_in[i, j] * old[j]
                    new = old[i] + tracer_step * growth
                    kept = jnp.where(is_wet, new, old[i])
                    if heated:
                        a = absorb_in[i]
                        heat_d = a * new if i == 0 else heat_d + a * new
                        heat_b = a * kept if i == 0 else heat_b + a * kept
                else:
                    new, kept = heat_d, heat_b
                react_d[n] = new
                base[n] = kept
                rows_send[turn, 0, pl.ds(n, 1)] = new[rows - 1 : rows]
                rows_send[turn, 1, pl.ds(n, 1)] = new[0:1]
                p, at = divmod(n, LANES)
                here = lane == at
                turned = pltpu.roll(new, (at + 1) % columns, 1)
                to_east[p] = jnp.where(here, turned, to_east[p])
                turned = pltpu.roll(new, at, 1) if at else new
                to_west[p] = jnp.where(here, turned, to_west[p])
        for p in range(len(to_east)):
            cols_send[turn, 0, p] = to_east[p]
            cols_send[turn, 1, p] = to_west[p]
        copies = []
        for i, d in enumerate((1, -1)):
            copies.append(
                remote(
                    rows_send.at[turn, i],
                    rows_recv.at[turn, i],
                    halo_ssem.at[turn, i],
                    halo_rsem.at[turn, i],
                    me_s,
                    steps_t[d],
                )
            )
            copies.append(
                remote(
                    cols_send.at[turn, i],
                    cols_recv.at[turn, i],
                    halo_ssem.at[turn, 2 + i],
                    halo_rsem.at[turn, 2 + i],
                    sect_at(1 if i == 0 else sects - 1),
                    me_t,
                )
            )
        for copy in copies:
            copy.start()
        sent.extend(copies)
        return copies, cells

    def shift_cells(turn, cells):
        from_west = [cols_recv[turn, 0, p] for p in range(pl.cdiv(cells, LANES))]
        from_east = [cols_recv[turn, 1, p] for p in range(pl.cdiv(cells, LANES))]
        for n in range(cells):
            p, at = divmod(n, LANES)
            new = react_d[n]
            edge = pltpu.roll(from_west[p], columns - at, 1) if at else from_west[p]
            west_v[n] = jnp.where(lane == 0, edge, pltpu.roll(new, 1, 1))
            edge = pltpu.roll(from_east[p], columns - 1 - at, 1) if at < columns - 1 else from_east[p]
            east_v[n] = jnp.where(lane == columns - 1, edge, pltpu.roll(new, columns - 1, 1))
            edge = jnp.broadcast_to(rows_recv[turn, 0, pl.ds(n, 1)], (rows, columns))
            south_v[n] = jnp.where(row == 0, edge, pltpu.roll(new, 1, 0))
            edge = jnp.broadcast_to(rows_recv[turn, 1, pl.ds(n, 1)], (rows, columns))
            north_v[n] = jnp.where(row == rows - 1, edge, pltpu.roll(new, rows - 1, 0))

    def send_means(turn, means):
        copies = []
        for l, pair in enumerate(means):
            for f, mean in enumerate(pair):
                for s in range(sects):
                    mean_send[turn, s, f, l] = mean[:, s * columns : (s + 1) * columns]
        for o in range(1, sects):
            to = sect_at(o)
            copies.append(
                remote(
                    mean_send.at[turn, to],
                    mean_recv.at[turn, me_s],
                    mean_ssem.at[turn, o],
                    mean_rsem.at[turn, o],
                    to,
                    me_t,
                )
            )
        for copy in copies:
            copy.start()
        sent.extend(copies)
        mean_recv[turn, me_s] = mean_send[turn, me_s]
        return copies

    def column_terms(turn):
        kappa, stencil = [], []
        half_wet = tracer_step * wet_cols
        for k in range(levels):
            along_x = mean_recv[turn, k // depth, 0, k % depth]
            along_y = mean_recv[turn, k // depth, 1, k % depth]
            kappa.append(kappa_in[k] * (1.0 + stir_gain * (along_x * along_x + along_y * along_y)))
            upwind = flags[k] == 1
            terms = []
            for speed in (along_x, along_y):
                terms.append(half_wet * jnp.where(upwind, jnp.maximum(speed, 0.0), 0.5 * speed))
                terms.append(half_wet * jnp.where(upwind, jnp.minimum(speed, 0.0), 0.5 * speed))
            stencil.append(terms)
        couple = [tracer_step * 0.5 * (kappa[k] + kappa[k + 1]) for k in range(levels - 1)]
        out, factor = [], None
        for k in range(levels):
            denom = 1.0
            if k > 0:
                denom = denom + couple[k - 1]
            if k < levels - 1:
                denom = denom + couple[k]
            if k > 0:
                denom = denom + couple[k - 1] * factor
            inverse = 1.0 / denom
            px, qx, py, qy = stencil[k]
            out.append(
                dict(
                    centre=inverse * (1.0 - ((px - qx) + (py - qy))),
                    west=inverse * px,
                    east=inverse * qx,
                    south=inverse * py,
                    north=inverse * qy,
                    lower=inverse * couple[k - 1] if k > 0 else None,
                    upper=inverse * couple[k] if k < levels - 1 else None,
                )
            )
            factor = -out[k]["upper"] if k < levels - 1 else None
        return out

    def tracer_column(terms, i):
        partial = []
        for k in range(levels):
            n = i * levels + k
            t = terms[k]
            now = (
                t["centre"] * base[n]
                + (t["west"] * west_v[n] - t["east"] * east_v[n])
                + (t["south"] * south_v[n] - t["north"] * north_v[n])
            )
            if k > 0:
                now = now + t["lower"] * partial[k - 1]
            partial.append(now)
        for k in range(levels - 2, -1, -1):
            partial[k] = partial[k] + terms[k]["upper"] * partial[k + 1]
        return partial

    halo0, cells0 = react_and_send(0, True)
    for copy in local[3:]:
        copy.wait()
    for copy in first:
        copy.wait_recv()
    wet = sea[...].astype(jnp.float32)
    means = []
    for l in range(depth):
        z, m, h, zm, mm = ocean_steps(
            ocean[0, 0, l], ocean[0, 1, l], ocean[0, 2, l], wet, None, rows
        )
        means.append((zm, mm))
        for f, value in enumerate((z, m, h)):
            state_send[f, l] = value
    got = send_means(0, means)
    state = []
    for i, d in enumerate((1, -1)):
        state.append(
            remote(
                state_send,
                ocean.at[1, :, :, slot(d)],
                state_ssem.at[i],
                state_rsem.at[i],
                me_s,
                steps_t[d],
            )
        )
    for copy in state:
        copy.start()
    sent.extend(state)
    for f in range(3):
        for l in range(depth):
            ocean[1, f, l, slot(0)] = state_send[f, l]
    for copy in halo0:
        copy.wait_recv()
    shift_cells(0, cells0)
    for copy in got:
        copy.wait_recv()
    terms = column_terms(0)

    heat = tracer_column(terms, tracers)
    for k in range(levels):
        heat_send[k // depth, k % depth] = light_in[k] * heat[k]
    heats = []
    for o in range(sects - 1, -1, -1):
        for i, d in enumerate((1, -1, 0)):
            if (o, d) == (0, 0):
                continue
            to = sect_at(o)
            heats.append(
                remote(
                    heat_send.at[to],
                    heat_recv.at[me_s, :, slot(d)],
                    heat_ssem.at[o, i],
                    heat_rsem.at[o, i],
                    to,
                    steps_t[d],
                )
            )
    for copy in heats:
        copy.start()
    sent.extend(heats)
    heat_recv[me_s, :, slot(0)] = heat_send[me_s]

    for i in range(tracers):
        for k, value in enumerate(tracer_column(terms, i)):
            conc[i, k] = value
    halo1, cells1 = react_and_send(1, False)
    for copy in halo1:
        copy.wait_recv()
    shift_cells(1, cells1)

    for copy in state:
        copy.wait_recv()
    for copy in heats:
        copy.wait_recv()
    means = []
    for l in range(depth):
        forcing = jnp.concatenate([heat_recv[s, l] for s in range(sects)], axis=1)
        z, m, h, zm, mm = ocean_steps(
            ocean[1, 0, l], ocean[1, 1, l], ocean[1, 2, l], wet, forcing, rows
        )
        means.append((zm, mm))
        zonal_out[l] = z
        merid_out[l] = m
        height_out[l] = h
    got = send_means(1, means)
    for copy in got:
        copy.wait_recv()
    terms = column_terms(1)
    for i in range(tracers):
        for k, value in enumerate(tracer_column(terms, i)):
            conc_out[i, k] = value
    for copy in sent:
        copy.wait_send()


def put_out(*refs):
    copies = [
        pltpu.make_async_copy(src, dst, refs[8].at[i])
        for i, (src, dst) in enumerate(zip(refs[:4], refs[4:8]))
    ]
    for copy in copies:
        copy.start()
    for copy in copies:
        copy.wait()


def body(sects, tiles, zonal, merid, height, level_kappa, sea, flags, conc, react, absorb, light):
    tracers, levels, rows, columns = conc.shape
    depth, _, wide = zonal.shape
    assert rows >= 2 * STEPS and columns % LANES == 0 and INTERVALS == 2
    cells = (tracers + 1) * levels
    packs = pl.cdiv(cells, LANES)
    padded = pl.cdiv(cells, 8) * 8
    f32 = jnp.float32
    dma = pltpu.SemaphoreType.DMA
    any_space = pl.BlockSpec(memory_space=pl.ANY)
    vmem = pl.BlockSpec(memory_space=pltpu.VMEM)
    results = pl.pallas_call(
        functools.partial(kernel, sects, tiles),
        out_shape=[
            pltpu.VMEM(conc.shape, f32),
            pltpu.VMEM(zonal.shape, f32),
            pltpu.VMEM(merid.shape, f32),
            pltpu.VMEM(height.shape, f32),
        ],
        in_specs=[pl.BlockSpec(memory_space=pltpu.HBM)] * 10,
        out_specs=[vmem] * 4,
        scratch_shapes=[
            pltpu.SMEM(level_kappa.shape, f32),
            pltpu.SMEM(react.shape, f32),
            pltpu.SMEM(absorb.shape, f32),
            pltpu.SMEM(light.shape, f32),
            pltpu.VMEM((2, 3, depth, 3 * rows, wide), f32),
            pltpu.VMEM((3 * rows, wide), jnp.int32),
            pltpu.VMEM(flags.shape, jnp.int32),
            pltpu.VMEM(conc.shape, f32),
        ]
        + [pltpu.VMEM((cells, rows, columns), f32)] * 6
        + [
            pltpu.VMEM((2, 2, packs, rows, columns), f32),
            pltpu.VMEM((2, 2, packs, rows, columns), f32),
            pltpu.VMEM((2, 2, padded, columns), f32),
            pltpu.VMEM((2, 2, padded, columns), f32),
            pltpu.VMEM((3, depth, rows, wide), f32),
            pltpu.VMEM((2, sects, 2, depth, rows, columns), f32),
            pltpu.VMEM((2, sects, 2, depth, rows, columns), f32),
            pltpu.VMEM((sects, depth, rows, columns), f32),
            pltpu.VMEM((sects, depth, 3 * rows, columns), f32),
            dma((10,)),
            dma((2, 4)),
            dma((2, 4)),
            dma((2,)),
            dma((2,)),
            dma((2, 4)),
            dma((2, 4)),
            dma((2, sects)),
            dma((2, sects)),
            dma((sects, 3)),
            dma((sects, 3)),
        ],
        compiler_params=pltpu.CompilerParams(collective_id=0, has_side_effects=True),
        name="coupled",
    )(zonal, merid, height, sea, flags, conc, level_kappa, react, absorb, light)
    return pl.pallas_call(
        put_out,
        out_shape=[jax.ShapeDtypeStruct(r.shape, f32) for r in results],
        in_specs=[vmem] * 4,
        out_specs=[any_space] * 4,
        scratch_shapes=[dma((4,))],
        name="put_out",
    )(*[pltpu.with_memory_space_constraint(r, pltpu.VMEM) for r in results])


def solution(mesh):
    placed = (
        P("sect", "tile", None),
        P("sect", "tile", None),
        P("sect", "tile", None),
        P(),
        P("tile", None),
        P(None, "tile", "sect"),
        P(None, None, "tile", "sect"),
        P(),
        P(),
        P(),
    )
    return jax.shard_map(
        functools.partial(body, mesh.shape["sect"], mesh.shape["tile"]),
        mesh=mesh,
        in_specs=placed,
        out_specs=(
            P(None, None, "tile", "sect"),
            P("sect", "tile", None),
            P("sect", "tile", None),
            P("sect", "tile", None),
        ),
        check_vma=False,
    )
```

```python
import functools

import jax
import jax.numpy as jnp
from jax import lax
from jax.experimental import pallas as pl
from jax.experimental.pallas import tpu as pltpu
from jax.sharding import PartitionSpec as P

STEPS = 4
INTERVALS = 2

time_step = 0.1
gravity = 1.0
coriolis = 0.3
viscosity = 0.05
heat_coupling = 0.05
tracer_step = 0.5
stir_gain = 4.0

LANES = 128


def ocean_steps(zonal, merid, height, wet, forcing, rows):
    tall, wide = zonal.shape

    def east(a):
        return pltpu.roll(a, wide - 1, 1)

    def west(a):
        return pltpu.roll(a, 1, 1)

    def north(a):
        return pltpu.roll(a, tall - 1, 0)

    def south(a):
        return pltpu.roll(a, 1, 0)

    own = slice(rows, 2 * rows)
    zonal_sum = jnp.zeros((rows, wide), jnp.float32)
    merid_sum = jnp.zeros((rows, wide), jnp.float32)
    for _ in range(STEPS):
        ze, zw, zn, zs = east(zonal), west(zonal), north(zonal), south(zonal)
        me, mw, mn, ms = east(merid), west(merid), north(merid), south(merid)
        height = height - (0.5 * time_step) * ((ze - zw) + (mn - ms))
        if forcing is not None:
            height = height + (time_step * heat_coupling) * forcing
        zonal_lap = zn + zs + ze + zw - 4.0 * zonal
        merid_lap = mn + ms + me + mw - 4.0 * merid
        zonal_new = wet * (
            zonal
            + time_step
            * (
                coriolis * merid
                - (0.5 * gravity) * (east(height) - west(height))
                + viscosity * zonal_lap
            )
        )
        merid_new = wet * (
            merid
            + time_step
            * (
                -coriolis * zonal
                - (0.5 * gravity) * (north(height) - south(height))
                + viscosity * merid_lap
            )
        )
        zonal, merid = zonal_new, merid_new
        zonal_sum = zonal_sum + zonal[own]
        merid_sum = merid_sum + merid[own]
    return zonal[own], merid[own], height[own], zonal_sum / STEPS, merid_sum / STEPS


def kernel(
    sects,
    tiles,
    zonal_in,
    merid_in,
    height_in,
    sea_in,
    flags_in,
    conc_in,
    kappa_hbm,
    react_hbm,
    absorb_hbm,
    light_hbm,
    conc_out,
    zonal_out,
    merid_out,
    height_out,
    kappa_in,
    react_in,
    absorb_in,
    light_in,
    ocean,
    sea,
    flags,
    conc,
    react_d,
    base,
    west_v,
    east_v,
    south_v,
    north_v,
    cols_send,
    cols_recv,
    rows_send,
    rows_recv,
    state_send,
    mean_send,
    mean_recv,
    heat_send,
    heat_recv,
    local_sem,
    first_send,
    first_recv,
    state_ssem,
    state_rsem,
    halo_ssem,
    halo_rsem,
    mean_ssem,
    mean_rsem,
    heat_ssem,
    heat_rsem,
    known_sem,
):
    me_s = lax.axis_index("sect")
    me_t = lax.axis_index("tile")
    tracers, levels, rows, columns = conc_in.shape
    depth = zonal_in.shape[0]
    above = lax.rem(me_t + 1, tiles)
    below = lax.rem(me_t + tiles - 1, tiles)
    steps_t = {1: above, 0: me_t, -1: below}

    def sect_at(offset):
        return lax.rem(me_s + offset, sects)

    def flipped(bit):
        step = 1 << bit
        return me_s + step - 2 * step * lax.rem(me_s // step, 2)

    def tell(bit):
        pl.semaphore_signal(
            known_sem.at[bit],
            inc=1,
            device_id=(flipped(bit), me_t),
            device_id_type=pl.DeviceIdType.MESH,
        )

    def hear_of_all():
        for b in range(bits - 1):
            pl.semaphore_wait(known_sem.at[b], 1)
            if b + 1 < bits - 1:
                tell(b + 1)

    def remote(src, dst, send, recv, to_s, to_t):
        return pltpu.make_async_remote_copy(
            src_ref=src,
            dst_ref=dst,
            send_sem=send,
            recv_sem=recv,
            device_id=(to_s, to_t),
            device_id_type=pl.DeviceIdType.MESH,
        )

    def slot(step):
        return pl.ds((1 - step) * rows, rows)

    fields_in = (zonal_in, merid_in, height_in)
    local = [
        pltpu.make_async_copy(conc_in, conc, local_sem.at[0]),
        pltpu.make_async_copy(flags_in, flags, local_sem.at[1]),
        pltpu.make_async_copy(sea_in, sea.at[slot(0)], local_sem.at[2]),
    ] + [
        pltpu.make_async_copy(field, ocean.at[0, f, :, slot(0)], local_sem.at[3 + f])
        for f, field in enumerate(fields_in)
    ]
    scalars = [
        pltpu.make_async_copy(src, dst, local_sem.at[6 + i])
        for i, (src, dst) in enumerate(
            (
                (react_hbm, react_in),
                (absorb_hbm, absorb_in),
                (kappa_hbm, kappa_in),
                (light_hbm, light_in),
            )
        )
    ]
    barrier = pltpu.get_barrier_semaphore()
    bits = sects.bit_length() - 1
    greeted = [(me_s, above), (me_s, below)] + [(flipped(b), me_t) for b in range(bits)]
    for peer in greeted:
        pl.semaphore_signal(
            barrier, inc=1, device_id=peer, device_id_type=pl.DeviceIdType.MESH
        )
    for copy in scalars + local:
        copy.start()
    pl.semaphore_wait(barrier, len(greeted))

    first = []
    for i, d in enumerate((1, -1)):
        for f, field in enumerate(fields_in):
            first.append(
                remote(
                    field,
                    ocean.at[0, f, :, slot(d)],
                    first_send.at[i, f],
                    first_recv.at[i, f],
                    me_s,
                    steps_t[d],
                )
            )
        first.append(
            remote(
                sea_in,
                sea.at[slot(d)],
                first_send.at[i, 3],
                first_recv.at[i, 3],
                me_s,
                steps_t[d],
            )
        )
    for copy in first:
        copy.start()
    if bits > 1:
        tell(0)
    sent = list(first)

    lane = lax.broadcasted_iota(jnp.int32, (rows, columns), 1)
    row = lax.broadcasted_iota(jnp.int32, (rows, columns), 0)

    for copy in scalars + local[:3]:
        copy.wait()
    own_columns = pl.ds(pl.multiple_of(me_s * columns, LANES), columns)
    sea_cols = sea[slot(0), own_columns]
    wet_cols = sea_cols.astype(jnp.float32)
    is_wet = sea_cols == 1

    def react_and_send(turn, heated):
        names = tracers + (1 if heated else 0)
        cells = names * levels
        to_east = [jnp.zeros((rows, columns), jnp.float32) for _ in range(pl.cdiv(cells, LANES))]
        to_west = list(to_east)
        for k in range(levels):
            old = [conc[i, k] for i in range(tracers)]
            heat_d = None
            for i in range(names):
                n = i * levels + k
                if i < tracers:
                    growth = react_in[i, 0] * old[0]
                    for j in range(1, tracers):
                        growth = growth + react_in[i, j] * old[j]
                    new = old[i] + tracer_step * growth
                    kept = jnp.where(is_wet, new, old[i])
                    if heated:
                        a = absorb_in[i]
                        heat_d = a * new if i == 0 else heat_d + a * new
                        heat_b = a * kept if i == 0 else heat_b + a * kept
                else:
                    new, kept = heat_d, heat_b
                react_d[n] = new
                base[n] = kept
                rows_send[turn, 0, pl.ds(n, 1)] = new[rows - 1 : rows]
                rows_send[turn, 1, pl.ds(n, 1)] = new[0:1]
                p, at = divmod(n, LANES)
                here = lane == at
                turned = pltpu.roll(new, (at + 1) % columns, 1)
                to_east[p] = jnp.where(here, turned, to_east[p])
                turned = pltpu.roll(new, at, 1) if at else new
                to_west[p] = jnp.where(here, turned, to_west[p])
        for p in range(len(to_east)):
            cols_send[turn, 0, p] = to_east[p]
            cols_send[turn, 1, p] = to_west[p]
        if turn == 0:
            hear_of_all()
        copies = []
        for i, d in enumerate((1, -1)):
            copies.append(
                remote(
                    rows_send.at[turn, i],
                    rows_recv.at[turn, i],
                    halo_ssem.at[turn, i],
                    halo_rsem.at[turn, i],
                    me_s,
                    steps_t[d],
                )
            )
            copies.append(
                remote(
                    cols_send.at[turn, i],
                    cols_recv.at[turn, i],
                    halo_ssem.at[turn, 2 + i],
                    halo_rsem.at[turn, 2 + i],
                    sect_at(1 if i == 0 else sects - 1),
                    me_t,
                )
            )
        for copy in copies:
            copy.start()
        sent.extend(copies)
        return copies, cells

    def shift_cells(turn, cells):
        from_west = [cols_recv[turn, 0, p] for p in range(pl.cdiv(cells, LANES))]
        from_east = [cols_recv[turn, 1, p] for p in range(pl.cdiv(cells, LANES))]
        for n in range(cells):
            p, at = divmod(n, LANES)
            new = react_d[n]
            edge = pltpu.roll(from_west[p], columns - at, 1) if at else from_west[p]
            west_v[n] = jnp.where(lane == 0, edge, pltpu.roll(new, 1, 1))
            edge = pltpu.roll(from_east[p], columns - 1 - at, 1) if at < columns - 1 else from_east[p]
            east_v[n] = jnp.where(lane == columns - 1, edge, pltpu.roll(new, columns - 1, 1))
            edge = jnp.broadcast_to(rows_recv[turn, 0, pl.ds(n, 1)], (rows, columns))
            south_v[n] = jnp.where(row == 0, edge, pltpu.roll(new, 1, 0))
            edge = jnp.broadcast_to(rows_recv[turn, 1, pl.ds(n, 1)], (rows, columns))
            north_v[n] = jnp.where(row == rows - 1, edge, pltpu.roll(new, rows - 1, 0))

    def send_means(turn, means):
        copies = []
        for l, pair in enumerate(means):
            for f, mean in enumerate(pair):
                for s in range(sects):
                    mean_send[turn, s, f, l] = mean[:, s * columns : (s + 1) * columns]
        for o in range(1, sects):
            to = sect_at(o)
            copies.append(
                remote(
                    mean_send.at[turn, to],
                    mean_recv.at[turn, me_s],
                    mean_ssem.at[turn, o],
                    mean_rsem.at[turn, o],
                    to,
                    me_t,
                )
            )
        for copy in copies:
            copy.start()
        sent.extend(copies)
        mean_recv[turn, me_s] = mean_send[turn, me_s]
        return copies

    def column_terms(turn):
        kappa, stencil = [], []
        half_wet = tracer_step * wet_cols
        for k in range(levels):
            along_x = mean_recv[turn, k // depth, 0, k % depth]
            along_y = mean_recv[turn, k // depth, 1, k % depth]
            kappa.append(kappa_in[k] * (1.0 + stir_gain * (along_x * along_x + along_y * along_y)))
            upwind = flags[k] == 1
            terms = []
            for speed in (along_x, along_y):
                terms.append(half_wet * jnp.where(upwind, jnp.maximum(speed, 0.0), 0.5 * speed))
                terms.append(half_wet * jnp.where(upwind, jnp.minimum(speed, 0.0), 0.5 * speed))
            stencil.append(terms)
        couple = [tracer_step * 0.5 * (kappa[k] + kappa[k + 1]) for k in range(levels - 1)]
        out, factor = [], None
        for k in range(levels):
            denom = 1.0
            if k > 0:
                denom = denom + couple[k - 1]
            if k < levels - 1:
                denom = denom + couple[k]
            if k > 0:
                denom = denom + couple[k - 1] * factor
            inverse = 1.0 / denom
            px, qx, py, qy = stencil[k]
            out.append(
                dict(
                    centre=inverse * (1.0 - ((px - qx) + (py - qy))),
                    west=inverse * px,
                    east=inverse * qx,
                    south=inverse * py,
                    north=inverse * qy,
                    lower=inverse * couple[k - 1] if k > 0 else None,
                    upper=inverse * couple[k] if k < levels - 1 else None,
                )
            )
            factor = -out[k]["upper"] if k < levels - 1 else None
        return out

    def tracer_column(terms, i):
        partial = []
        for k in range(levels):
            n = i * levels + k
            t = terms[k]
            now = (
                t["centre"] * base[n]
                + (t["west"] * west_v[n] - t["east"] * east_v[n])
                + (t["south"] * south_v[n] - t["north"] * north_v[n])
            )
            if k > 0:
                now = now + t["lower"] * partial[k - 1]
            partial.append(now)
        for k in range(levels - 2, -1, -1):
            partial[k] = partial[k] + terms[k]["upper"] * partial[k + 1]
        return partial

    halo0, cells0 = react_and_send(0, True)
    for copy in local[3:]:
        copy.wait()
    for copy in first:
        copy.wait_recv()
    wet = sea[...].astype(jnp.float32)
    means = []
    for l in range(depth):
        z, m, h, zm, mm = ocean_steps(
            ocean[0, 0, l], ocean[0, 1, l], ocean[0, 2, l], wet, None, rows
        )
        means.append((zm, mm))
        for f, value in enumerate((z, m, h)):
            state_send[f, l] = value
    got = send_means(0, means)
    state = []
    for i, d in enumerate((1, -1)):
        state.append(
            remote(
                state_send,
                ocean.at[1, :, :, slot(d)],
                state_ssem.at[i],
                state_rsem.at[i],
                me_s,
                steps_t[d],
            )
        )
    for copy in state:
        copy.start()
    sent.extend(state)
    for f in range(3):
        for l in range(depth):
            ocean[1, f, l, slot(0)] = state_send[f, l]
    for copy in halo0:
        copy.wait_recv()
    shift_cells(0, cells0)
    for copy in got:
        copy.wait_recv()
    terms = column_terms(0)

    heat = tracer_column(terms, tracers)
    for k in range(levels):
        heat_send[k // depth, k % depth] = light_in[k] * heat[k]
    heats = []
    for o in range(sects - 1, -1, -1):
        for i, d in enumerate((1, -1, 0)):
            if (o, d) == (0, 0):
                continue
            to = sect_at(o)
            heats.append(
                remote(
                    heat_send.at[to],
                    heat_recv.at[me_s, :, slot(d)],
                    heat_ssem.at[o, i],
                    heat_rsem.at[o, i],
                    to,
                    steps_t[d],
                )
            )
    for copy in heats:
        copy.start()
    sent.extend(heats)
    heat_recv[me_s, :, slot(0)] = heat_send[me_s]

    for i in range(tracers):
        for k, value in enumerate(tracer_column(terms, i)):
            conc[i, k] = value
    halo1, cells1 = react_and_send(1, False)
    for copy in state:
        copy.wait_recv()
    for copy in heats:
        copy.wait_recv()
    means = []
    for l in range(depth):
        forcing = jnp.concatenate([heat_recv[s, l] for s in range(sects)], axis=1)
        z, m, h, zm, mm = ocean_steps(
            ocean[1, 0, l], ocean[1, 1, l], ocean[1, 2, l], wet, forcing, rows
        )
        means.append((zm, mm))
        zonal_out[l] = z
        merid_out[l] = m
        height_out[l] = h
    got = send_means(1, means)
    for copy in halo1:
        copy.wait_recv()
    shift_cells(1, cells1)
    for copy in got:
        copy.wait_recv()
    terms = column_terms(1)
    for i in range(tracers):
        for k, value in enumerate(tracer_column(terms, i)):
            conc_out[i, k] = value
    for copy in sent:
        copy.wait_send()


def put_out(*refs):
    copies = [
        pltpu.make_async_copy(src, dst, refs[8].at[i])
        for i, (src, dst) in enumerate(zip(refs[:4], refs[4:8]))
    ]
    for copy in copies:
        copy.start()
    for copy in copies:
        copy.wait()


def body(sects, tiles, zonal, merid, height, level_kappa, sea, flags, conc, react, absorb, light):
    tracers, levels, rows, columns = conc.shape
    depth, _, wide = zonal.shape
    assert sects & (sects - 1) == 0 and rows >= 2 * STEPS and columns % LANES == 0 and INTERVALS == 2
    cells = (tracers + 1) * levels
    packs = pl.cdiv(cells, LANES)
    padded = pl.cdiv(cells, 8) * 8
    f32 = jnp.float32
    dma = pltpu.SemaphoreType.DMA
    any_space = pl.BlockSpec(memory_space=pl.ANY)
    vmem = pl.BlockSpec(memory_space=pltpu.VMEM)
    results = pl.pallas_call(
        functools.partial(kernel, sects, tiles),
        out_shape=[
            pltpu.VMEM(conc.shape, f32),
            pltpu.VMEM(zonal.shape, f32),
            pltpu.VMEM(merid.shape, f32),
            pltpu.VMEM(height.shape, f32),
        ],
        in_specs=[pl.BlockSpec(memory_space=pltpu.HBM)] * 10,
        out_specs=[vmem] * 4,
        scratch_shapes=[
            pltpu.SMEM(level_kappa.shape, f32),
            pltpu.SMEM(react.shape, f32),
            pltpu.SMEM(absorb.shape, f32),
            pltpu.SMEM(light.shape, f32),
            pltpu.VMEM((2, 3, depth, 3 * rows, wide), f32),
            pltpu.VMEM((3 * rows, wide), jnp.int32),
            pltpu.VMEM(flags.shape, jnp.int32),
            pltpu.VMEM(conc.shape, f32),
        ]
        + [pltpu.VMEM((cells, rows, columns), f32)] * 6
        + [
            pltpu.VMEM((2, 2, packs, rows, columns), f32),
            pltpu.VMEM((2, 2, packs, rows, columns), f32),
            pltpu.VMEM((2, 2, padded, columns), f32),
            pltpu.VMEM((2, 2, padded, columns), f32),
            pltpu.VMEM((3, depth, rows, wide), f32),
            pltpu.VMEM((2, sects, 2, depth, rows, columns), f32),
            pltpu.VMEM((2, sects, 2, depth, rows, columns), f32),
            pltpu.VMEM((sects, depth, rows, columns), f32),
            pltpu.VMEM((sects, depth, 3 * rows, columns), f32),
            dma((10,)),
            dma((2, 4)),
            dma((2, 4)),
            dma((2,)),
            dma((2,)),
            dma((2, 4)),
            dma((2, 4)),
            dma((2, sects)),
            dma((2, sects)),
            dma((sects, 3)),
            dma((sects, 3)),
            pltpu.SemaphoreType.REGULAR((max(sects.bit_length() - 2, 1),)),
        ],
        compiler_params=pltpu.CompilerParams(collective_id=0, has_side_effects=True),
        name="coupled",
    )(zonal, merid, height, sea, flags, conc, level_kappa, react, absorb, light)
    return pl.pallas_call(
        put_out,
        out_shape=[jax.ShapeDtypeStruct(r.shape, f32) for r in results],
        in_specs=[vmem] * 4,
        out_specs=[any_space] * 4,
        scratch_shapes=[dma((4,))],
        name="put_out",
    )(*[pltpu.with_memory_space_constraint(r, pltpu.VMEM) for r in results])


def solution(mesh):
    placed = (
        P("sect", "tile", None),
        P("sect", "tile", None),
        P("sect", "tile", None),
        P(),
        P("tile", None),
        P(None, "tile", "sect"),
        P(None, None, "tile", "sect"),
        P(),
        P(),
        P(),
    )
    return jax.shard_map(
        functools.partial(body, mesh.shape["sect"], mesh.shape["tile"]),
        mesh=mesh,
        in_specs=placed,
        out_specs=(
            P(None, None, "tile", "sect"),
            P("sect", "tile", None),
            P("sect", "tile", None),
            P("sect", "tile", None),
        ),
        check_vma=False,
    )
```

```python
import functools

import jax
import jax.numpy as jnp
from jax import lax
from jax.experimental import pallas as pl
from jax.experimental.pallas import tpu as pltpu
from jax.sharding import PartitionSpec as P

STEPS = 4
INTERVALS = 2

time_step = 0.1
gravity = 1.0
coriolis = 0.3
viscosity = 0.05
heat_coupling = 0.05
tracer_step = 0.5
stir_gain = 4.0

LANES = 128


def ocean_steps(zonal, merid, height, wet, heating, rows):
    tall, wide = zonal.shape

    def east(a):
        return pltpu.roll(a, wide - 1, 1)

    def west(a):
        return pltpu.roll(a, 1, 1)

    def north(a):
        return pltpu.roll(a, tall - 1, 0)

    def south(a):
        return pltpu.roll(a, 1, 0)

    own = slice(rows, 2 * rows)
    zonal_sum = jnp.zeros((rows, wide), jnp.float32)
    merid_sum = jnp.zeros((rows, wide), jnp.float32)
    for step in range(STEPS):
        ze, zw, zn, zs = east(zonal), west(zonal), north(zonal), south(zonal)
        me, mw, mn, ms = east(merid), west(merid), north(merid), south(merid)
        height = height - (0.5 * time_step) * ((ze - zw) + (mn - ms))
        zonal_lap = zn + zs + ze + zw - 4.0 * zonal
        merid_lap = mn + ms + me + mw - 4.0 * merid
        zonal_part = zonal + time_step * (coriolis * merid + viscosity * zonal_lap)
        merid_part = merid + time_step * (-coriolis * zonal + viscosity * merid_lap)
        if heating is not None:
            if step == 0:
                forced = (time_step * heat_coupling) * heating()
            height = height + forced
        slope = 0.5 * gravity * time_step
        zonal_new = wet * (zonal_part - slope * (east(height) - west(height)))
        merid_new = wet * (merid_part - slope * (north(height) - south(height)))
        zonal, merid = zonal_new, merid_new
        zonal_sum = zonal_sum + zonal[own]
        merid_sum = merid_sum + merid[own]
    return zonal[own], merid[own], height[own], zonal_sum / STEPS, merid_sum / STEPS


def kernel(
    sects,
    tiles,
    zonal_in,
    merid_in,
    height_in,
    sea_in,
    flags_in,
    conc_in,
    kappa_hbm,
    react_hbm,
    absorb_hbm,
    light_hbm,
    conc_out,
    zonal_out,
    merid_out,
    height_out,
    kappa_in,
    react_in,
    absorb_in,
    light_in,
    ocean,
    sea,
    flags,
    conc,
    react_d,
    base,
    west_v,
    east_v,
    south_v,
    north_v,
    cols_send,
    cols_recv,
    rows_send,
    rows_recv,
    state_send,
    mean_send,
    mean_recv,
    heat_send,
    heat_recv,
    local_sem,
    first_send,
    first_recv,
    state_ssem,
    state_rsem,
    halo_ssem,
    halo_rsem,
    mean_ssem,
    mean_rsem,
    heat_ssem,
    heat_rsem,
    known_sem,
):
    me_s = lax.axis_index("sect")
    me_t = lax.axis_index("tile")
    tracers, levels, rows, columns = conc_in.shape
    depth = zonal_in.shape[0]
    above = lax.rem(me_t + 1, tiles)
    below = lax.rem(me_t + tiles - 1, tiles)
    steps_t = {1: above, 0: me_t, -1: below}

    def sect_at(offset):
        return lax.rem(me_s + offset, sects)

    def flipped(bit):
        step = 1 << bit
        return me_s + step - 2 * step * lax.rem(me_s // step, 2)

    def tell(bit):
        pl.semaphore_signal(
            known_sem.at[bit],
            inc=1,
            device_id=(flipped(bit), me_t),
            device_id_type=pl.DeviceIdType.MESH,
        )

    def hear_of_all():
        for b in range(bits - 1):
            pl.semaphore_wait(known_sem.at[b], 1)
            if b + 1 < bits - 1:
                tell(b + 1)

    def remote(src, dst, send, recv, to_s, to_t):
        return pltpu.make_async_remote_copy(
            src_ref=src,
            dst_ref=dst,
            send_sem=send,
            recv_sem=recv,
            device_id=(to_s, to_t),
            device_id_type=pl.DeviceIdType.MESH,
        )

    def slot(step):
        return pl.ds((1 - step) * rows, rows)

    fields_in = (zonal_in, merid_in, height_in)
    local = [
        pltpu.make_async_copy(conc_in, conc, local_sem.at[0]),
        pltpu.make_async_copy(flags_in, flags, local_sem.at[1]),
        pltpu.make_async_copy(sea_in, sea.at[slot(0)], local_sem.at[2]),
    ] + [
        pltpu.make_async_copy(field, ocean.at[0, f, :, slot(0)], local_sem.at[3 + f])
        for f, field in enumerate(fields_in)
    ]
    scalars = [
        pltpu.make_async_copy(src, dst, local_sem.at[6 + i])
        for i, (src, dst) in enumerate(
            (
                (react_hbm, react_in),
                (absorb_hbm, absorb_in),
                (kappa_hbm, kappa_in),
                (light_hbm, light_in),
            )
        )
    ]
    barrier = pltpu.get_barrier_semaphore()
    bits = sects.bit_length() - 1
    greeted = [(me_s, above), (me_s, below)] + [(flipped(b), me_t) for b in range(bits)]
    for peer in greeted:
        pl.semaphore_signal(
            barrier, inc=1, device_id=peer, device_id_type=pl.DeviceIdType.MESH
        )
    for copy in scalars + local:
        copy.start()
    pl.semaphore_wait(barrier, len(greeted))

    first = []
    for i, d in enumerate((1, -1)):
        for f, field in enumerate(fields_in):
            first.append(
                remote(
                    field,
                    ocean.at[0, f, :, slot(d)],
                    first_send.at[i, f],
                    first_recv.at[i, f],
                    me_s,
                    steps_t[d],
                )
            )
        first.append(
            remote(
                sea_in,
                sea.at[slot(d)],
                first_send.at[i, 3],
                first_recv.at[i, 3],
                me_s,
                steps_t[d],
            )
        )
    for copy in first:
        copy.start()
    if bits > 1:
        tell(0)
    sent = list(first)

    lane = lax.broadcasted_iota(jnp.int32, (rows, columns), 1)
    row = lax.broadcasted_iota(jnp.int32, (rows, columns), 0)

    for copy in scalars + local[:3]:
        copy.wait()
    own_columns = pl.ds(pl.multiple_of(me_s * columns, LANES), columns)
    sea_cols = sea[slot(0), own_columns]
    wet_cols = sea_cols.astype(jnp.float32)
    is_wet = sea_cols == 1

    def react_and_pack(turn, heated):
        names = tracers + (1 if heated else 0)
        cells = names * levels
        to_east = [jnp.zeros((rows, columns), jnp.float32) for _ in range(pl.cdiv(cells, LANES))]
        to_west = list(to_east)
        for k in range(levels):
            old = [conc[i, k] for i in range(tracers)]
            heat_d = None
            for i in range(names):
                n = i * levels + k
                if i < tracers:
                    growth = react_in[i, 0] * old[0]
                    for j in range(1, tracers):
                        growth = growth + react_in[i, j] * old[j]
                    new = old[i] + tracer_step * growth
                    kept = jnp.where(is_wet, new, old[i])
                    if heated:
                        a = absorb_in[i]
                        heat_d = a * new if i == 0 else heat_d + a * new
                        heat_b = a * kept if i == 0 else heat_b + a * kept
                else:
                    new, kept = heat_d, heat_b
                react_d[n] = new
                base[n] = kept
                rows_send[turn, 0, pl.ds(n, 1)] = new[rows - 1 : rows]
                rows_send[turn, 1, pl.ds(n, 1)] = new[0:1]
                p, at = divmod(n, LANES)
                here = lane == at
                turned = pltpu.roll(new, (at + 1) % columns, 1)
                to_east[p] = jnp.where(here, turned, to_east[p])
                turned = pltpu.roll(new, at, 1) if at else new
                to_west[p] = jnp.where(here, turned, to_west[p])
        for p in range(len(to_east)):
            cols_send[turn, 0, p] = to_east[p]
            cols_send[turn, 1, p] = to_west[p]
        copies = []
        for i, d in enumerate((1, -1)):
            copies.append(
                remote(
                    rows_send.at[turn, i],
                    rows_recv.at[turn, i],
                    halo_ssem.at[turn, i],
                    halo_rsem.at[turn, i],
                    me_s,
                    steps_t[d],
                )
            )
            copies.append(
                remote(
                    cols_send.at[turn, i],
                    cols_recv.at[turn, i],
                    halo_ssem.at[turn, 2 + i],
                    halo_rsem.at[turn, 2 + i],
                    sect_at(1 if i == 0 else sects - 1),
                    me_t,
                )
            )
        return copies, cells

    def shift_cells(turn, cells):
        from_west = [cols_recv[turn, 0, p] for p in range(pl.cdiv(cells, LANES))]
        from_east = [cols_recv[turn, 1, p] for p in range(pl.cdiv(cells, LANES))]
        for n in range(cells):
            p, at = divmod(n, LANES)
            new = react_d[n]
            edge = pltpu.roll(from_west[p], columns - at, 1) if at else from_west[p]
            west_v[n] = jnp.where(lane == 0, edge, pltpu.roll(new, 1, 1))
            edge = pltpu.roll(from_east[p], columns - 1 - at, 1) if at < columns - 1 else from_east[p]
            east_v[n] = jnp.where(lane == columns - 1, edge, pltpu.roll(new, columns - 1, 1))
            edge = jnp.broadcast_to(rows_recv[turn, 0, pl.ds(n, 1)], (rows, columns))
            south_v[n] = jnp.where(row == 0, edge, pltpu.roll(new, 1, 0))
            edge = jnp.broadcast_to(rows_recv[turn, 1, pl.ds(n, 1)], (rows, columns))
            north_v[n] = jnp.where(row == rows - 1, edge, pltpu.roll(new, rows - 1, 0))

    def send_means(turn, means):
        copies = []
        for l, pair in enumerate(means):
            for f, mean in enumerate(pair):
                for s in range(sects):
                    mean_send[turn, s, f, l] = mean[:, s * columns : (s + 1) * columns]
        for o in range(1, sects):
            to = sect_at(o)
            copies.append(
                remote(
                    mean_send.at[turn, to],
                    mean_recv.at[turn, me_s],
                    mean_ssem.at[turn, o],
                    mean_rsem.at[turn, o],
                    to,
                    me_t,
                )
            )
        for copy in copies:
            copy.start()
        sent.extend(copies)
        mean_recv[turn, me_s] = mean_send[turn, me_s]
        return copies

    def column_terms(turn):
        kappa, stencil = [], []
        half_wet = tracer_step * wet_cols
        for k in range(levels):
            along_x = mean_recv[turn, k // depth, 0, k % depth]
            along_y = mean_recv[turn, k // depth, 1, k % depth]
            kappa.append(kappa_in[k] * (1.0 + stir_gain * (along_x * along_x + along_y * along_y)))
            upwind = flags[k] == 1
            terms = []
            for speed in (along_x, along_y):
                terms.append(half_wet * jnp.where(upwind, jnp.maximum(speed, 0.0), 0.5 * speed))
                terms.append(half_wet * jnp.where(upwind, jnp.minimum(speed, 0.0), 0.5 * speed))
            stencil.append(terms)
        couple = [tracer_step * 0.5 * (kappa[k] + kappa[k + 1]) for k in range(levels - 1)]
        out, factor = [], None
        for k in range(levels):
            denom = 1.0
            if k > 0:
                denom = denom + couple[k - 1]
            if k < levels - 1:
                denom = denom + couple[k]
            if k > 0:
                denom = denom + couple[k - 1] * factor
            inverse = 1.0 / denom
            px, qx, py, qy = stencil[k]
            out.append(
                dict(
                    centre=inverse * (1.0 - ((px - qx) + (py - qy))),
                    west=inverse * px,
                    east=inverse * qx,
                    south=inverse * py,
                    north=inverse * qy,
                    lower=inverse * couple[k - 1] if k > 0 else None,
                    upper=inverse * couple[k] if k < levels - 1 else None,
                )
            )
            factor = -out[k]["upper"] if k < levels - 1 else None
        return out

    def tracer_column(terms, i):
        partial = []
        for k in range(levels):
            n = i * levels + k
            t = terms[k]
            now = (
                t["centre"] * base[n]
                + (t["west"] * west_v[n] - t["east"] * east_v[n])
                + (t["south"] * south_v[n] - t["north"] * north_v[n])
            )
            if k > 0:
                now = now + t["lower"] * partial[k - 1]
            partial.append(now)
        for k in range(levels - 2, -1, -1):
            partial[k] = partial[k] + terms[k]["upper"] * partial[k + 1]
        return partial

    halo0, cells0 = react_and_pack(0, True)
    for copy in local[3:]:
        copy.wait()
    for copy in first:
        copy.wait_recv()
    hear_of_all()
    for copy in halo0:
        copy.start()
    sent.extend(halo0)
    wet = sea[...].astype(jnp.float32)
    means = []
    for l in range(depth):
        z, m, h, zm, mm = ocean_steps(
            ocean[0, 0, l], ocean[0, 1, l], ocean[0, 2, l], wet, None, rows
        )
        means.append((zm, mm))
        for f, value in enumerate((z, m, h)):
            state_send[f, l] = value
    got = send_means(0, means)
    state = []
    for i, d in enumerate((1, -1)):
        state.append(
            remote(
                state_send,
                ocean.at[1, :, :, slot(d)],
                state_ssem.at[i],
                state_rsem.at[i],
                me_s,
                steps_t[d],
            )
        )
    for copy in state:
        copy.start()
    sent.extend(state)
    for f in range(3):
        for l in range(depth):
            ocean[1, f, l, slot(0)] = state_send[f, l]
    for copy in halo0:
        copy.wait_recv()
    shift_cells(0, cells0)
    for copy in got:
        copy.wait_recv()
    terms = column_terms(0)

    heat = tracer_column(terms, tracers)
    for k in range(levels):
        heat_send[k // depth, k % depth] = light_in[k] * heat[k]
    heats = []
    for o in range(sects - 1, -1, -1):
        for i, d in enumerate((1, -1, 0)):
            if (o, d) == (0, 0):
                continue
            to = sect_at(o)
            heats.append(
                remote(
                    heat_send.at[to],
                    heat_recv.at[me_s, :, slot(d)],
                    heat_ssem.at[o, i],
                    heat_rsem.at[o, i],
                    to,
                    steps_t[d],
                )
            )
    for copy in heats:
        copy.start()
    sent.extend(heats)
    heat_recv[me_s, :, slot(0)] = heat_send[me_s]

    for i in range(tracers):
        for k, value in enumerate(tracer_column(terms, i)):
            conc[i, k] = value
    halo1, cells1 = react_and_pack(1, False)
    for copy in halo1:
        copy.start()
    sent.extend(halo1)
    for copy in state:
        copy.wait_recv()

    def heating(l):
        if l == 0:
            for copy in heats:
                copy.wait_recv()
        return jnp.concatenate([heat_recv[s, l] for s in range(sects)], axis=1)

    means = []
    for l in range(depth):
        z, m, h, zm, mm = ocean_steps(
            ocean[1, 0, l], ocean[1, 1, l], ocean[1, 2, l], wet, functools.partial(heating, l), rows
        )
        means.append((zm, mm))
        zonal_out[l] = z
        merid_out[l] = m
        height_out[l] = h
    got = send_means(1, means)
    for copy in halo1:
        copy.wait_recv()
    shift_cells(1, cells1)
    for copy in got:
        copy.wait_recv()
    terms = column_terms(1)
    for i in range(tracers):
        for k, value in enumerate(tracer_column(terms, i)):
            conc_out[i, k] = value
    for copy in sent:
        copy.wait_send()


def put_out(*refs):
    copies = [
        pltpu.make_async_copy(src, dst, refs[8].at[i])
        for i, (src, dst) in enumerate(zip(refs[:4], refs[4:8]))
    ]
    for copy in copies:
        copy.start()
    for copy in copies:
        copy.wait()


def body(sects, tiles, zonal, merid, height, level_kappa, sea, flags, conc, react, absorb, light):
    tracers, levels, rows, columns = conc.shape
    depth, _, wide = zonal.shape
    assert sects & (sects - 1) == 0 and rows >= 2 * STEPS and columns % LANES == 0 and INTERVALS == 2
    cells = (tracers + 1) * levels
    packs = pl.cdiv(cells, LANES)
    padded = pl.cdiv(cells, 8) * 8
    f32 = jnp.float32
    dma = pltpu.SemaphoreType.DMA
    any_space = pl.BlockSpec(memory_space=pl.ANY)
    vmem = pl.BlockSpec(memory_space=pltpu.VMEM)
    results = pl.pallas_call(
        functools.partial(kernel, sects, tiles),
        out_shape=[
            pltpu.VMEM(conc.shape, f32),
            pltpu.VMEM(zonal.shape, f32),
            pltpu.VMEM(merid.shape, f32),
            pltpu.VMEM(height.shape, f32),
        ],
        in_specs=[pl.BlockSpec(memory_space=pltpu.HBM)] * 10,
        out_specs=[vmem] * 4,
        scratch_shapes=[
            pltpu.SMEM(level_kappa.shape, f32),
            pltpu.SMEM(react.shape, f32),
            pltpu.SMEM(absorb.shape, f32),
            pltpu.SMEM(light.shape, f32),
            pltpu.VMEM((2, 3, depth, 3 * rows, wide), f32),
            pltpu.VMEM((3 * rows, wide), jnp.int32),
            pltpu.VMEM(flags.shape, jnp.int32),
            pltpu.VMEM(conc.shape, f32),
        ]
        + [pltpu.VMEM((cells, rows, columns), f32)] * 6
        + [
            pltpu.VMEM((2, 2, packs, rows, columns), f32),
            pltpu.VMEM((2, 2, packs, rows, columns), f32),
            pltpu.VMEM((2, 2, padded, columns), f32),
            pltpu.VMEM((2, 2, padded, columns), f32),
            pltpu.VMEM((3, depth, rows, wide), f32),
            pltpu.VMEM((2, sects, 2, depth, rows, columns), f32),
            pltpu.VMEM((2, sects, 2, depth, rows, columns), f32),
            pltpu.VMEM((sects, depth, rows, columns), f32),
            pltpu.VMEM((sects, depth, 3 * rows, columns), f32),
            dma((10,)),
            dma((2, 4)),
            dma((2, 4)),
            dma((2,)),
            dma((2,)),
            dma((2, 4)),
            dma((2, 4)),
            dma((2, sects)),
            dma((2, sects)),
            dma((sects, 3)),
            dma((sects, 3)),
            pltpu.SemaphoreType.REGULAR((max(sects.bit_length() - 2, 1),)),
        ],
        compiler_params=pltpu.CompilerParams(collective_id=0, has_side_effects=True),
        name="coupled",
    )(zonal, merid, height, sea, flags, conc, level_kappa, react, absorb, light)
    return pl.pallas_call(
        put_out,
        out_shape=[jax.ShapeDtypeStruct(r.shape, f32) for r in results],
        in_specs=[vmem] * 4,
        out_specs=[any_space] * 4,
        scratch_shapes=[dma((4,))],
        name="put_out",
    )(*[pltpu.with_memory_space_constraint(r, pltpu.VMEM) for r in results])


def solution(mesh):
    placed = (
        P("sect", "tile", None),
        P("sect", "tile", None),
        P("sect", "tile", None),
        P(),
        P("tile", None),
        P(None, "tile", "sect"),
        P(None, None, "tile", "sect"),
        P(),
        P(),
        P(),
    )
    return jax.shard_map(
        functools.partial(body, mesh.shape["sect"], mesh.shape["tile"]),
        mesh=mesh,
        in_specs=placed,
        out_specs=(
            P(None, None, "tile", "sect"),
            P("sect", "tile", None),
            P("sect", "tile", None),
            P("sect", "tile", None),
        ),
        check_vma=False,
    )
```
